128 devices in a mesh: dp: 8 (over x, core), fsdp: 16 (over z, y).
Axes of the slice: x: 4, y: 4, z: 4, core: 2. Of those that a mesh axis runs over, the one named last changes fastest.
Arguments:
- hidden_rows: bfloat16 [2048, 15360], P('fsdp', 'dp'), may hold values from -6 to 6
- upstream: bfloat16 [2048, 4096], P('fsdp'), may hold values from -6 to 6
- advantages: float32 [16, 4], P('fsdp'), may hold values from -4 to 4
- lengths: int32 [16, 4], P('fsdp'), may hold values from 1 to 64, 128 in all within a row
- dest_rank: int32 [256, 1], P('fsdp'), may hold values from 0 to 15; in each aligned block of 16 rows (0 to 15, 16 to 31, ...) at most 2 rows name the same one
- w_down: bfloat16 [15360, 4096], P('dp', 'fsdp'), may hold values from -0.046875 to 0.046875
Outputs:
- packed_out: bfloat16 [4096, 4096], P('fsdp', 'dp')
- packed_back: bfloat16 [4096, 15360], P('fsdp', 'dp')
- weight_grad: float32 [15360, 4096], P('dp', 'fsdp')
The draws below stay inside these ranges and needn't reach their ends.
Inputs may be any that keep to these rules, and one draw needn't show every extreme that they name: Each generator group's 4 lengths sum to 128, the largest is 64. `dest_rank`: among the 16 blocks of one generator group, at most 2 name the same learner rank, and some learner is named 2 times.
All inputs are finite; a program needn't handle non-finite values.
Results may differ from the reference program's by a relative error of at most 0.014.
Values may be sent and summed in bfloat16 or wider, within the bound.
No kernel may reach another device: no remote copies, remote signals or barrier semaphores. Data moves between devices by JAX's collectives and lax.ppermute only.
A program may use at most 128 MiB of HBM per device.

```python
import math
import jax
import jax.numpy as jnp
import numpy as np
from jax import lax

D = 4096
FFW = 15360
S_DEV = 128
RPG = 4
SRC_BLOCKS = 16
SENDB = 2
MOSTLEN = 64
ROWS = 2048
BLOCKS_ALL = 256
N_DP = 8
N_FSDP = 16


def levels(rng, shape, shards, least, high):
    gain = 1.0
    for dim, parts in shards:
        draws = jax.random.uniform(jax.random.fold_in(jax.random.fold_in(rng, 6), dim), (parts,), jnp.float32, least / len(shards), high / len(shards))
        gain = gain * jnp.repeat(jnp.exp(draws), shape[dim] // parts).reshape((-1,) + (1,) * (len(shape) - 1 - dim))
    return gain


def length_profile(number_of, total, limit, lean):
    loads = [(1 << 20) // math.isqrt(grade ** lean) + 1 for grade in range(2, number_of + 1)]
    spare, holding = total - limit - (number_of - 1), [1] * (number_of - 1)
    while spare > 0:
        free = [i for i in range(number_of - 1) if holding[i] < limit]
        whole, left = sum([loads[i] for i in free]), spare
        for i in free:
            more = min(limit - holding[i], max(1, left * loads[i] // whole), spare)
            holding[i] = holding[i] + more
            spare = spare - more
    return np.array([limit] + holding)


def uneven(own_key, count, total, bound, skew):
    if count == 2:
        one = jax.random.randint(own_key, (), max(1, total - bound), min(bound, total - 1) + 1)
        return jnp.stack([one, total - one])
    tallies = jnp.asarray(length_profile(count, total, bound, skew), jnp.int32)
    twos = (count - 1) // 2
    giver, sink = tallies[1:1 + 2 * twos:2], tallies[2:2 + 2 * twos:2]
    slack = jnp.minimum(giver - 1, bound - sink)
    passed = jax.random.randint(jax.random.fold_in(own_key, 1), (twos,), 0, 1 << 20) % (slack + 1)
    tallies = tallies.at[1:1 + 2 * twos:2].set(giver - passed).at[2:2 + 2 * twos:2].set(sink + passed)
    return tallies[jax.random.permutation(jax.random.fold_in(own_key, 2), count)]


def deal_out(own_key, own, number, rows, amount, top, bound, slope):
    order = jax.random.permutation(own_key, amount)
    crowded, common = portions_of(amount, rows * top, bound, slope, True), portions_of(amount, rows * top, bound, slope, False)
    places = jnp.arange(amount)

    def named(sizes, offset_by):
        used = int((sizes > 0).sum())
        fixed = max(1, used // 4)
        moved = fixed + (places - fixed + offset_by * (used - fixed)) % max(1, amount - fixed)
        return jnp.zeros((amount,), jnp.int32).at[order[jnp.where(places < fixed, places, moved)]].set(jnp.asarray(sizes, jnp.int32))

    sizes = jnp.where(number % 4 == 0, named(crowded, number // 4), named(common, number - number // 4 - 1))
    mixed = jax.random.permutation(jax.random.fold_in(own, 3), amount)
    donor, sink = mixed[0:amount // 2 * 2:2], mixed[1:amount // 2 * 2:2]
    margin = jnp.minimum(sizes[donor] - 1, bound - sizes[sink]) // 2
    margin = jnp.where((donor == order[0]) | (sink == order[0]) | (sizes[sink] == 0), 0, jnp.maximum(margin, 0))
    moved = jax.random.randint(jax.random.fold_in(own, 4), (amount // 2,), 0, 1 << 20) % (margin + 1)
    sizes = sizes.at[donor].add(-moved).at[sink].add(moved)
    members = jnp.searchsorted(jnp.cumsum(sizes), jnp.arange(rows * top), side="right").astype(jnp.int32)
    table = members.reshape(top, rows).T
    table = table[jax.random.permutation(jax.random.fold_in(own, 1), rows)]
    offset_by = jax.random.randint(jax.random.fold_in(own, 2), (rows, 1), 0, top)
    return jnp.take_along_axis(table, (jnp.arange(top)[None, :] + offset_by) % top, axis=1)


def portions_of(number_of, total, reach, lean, full):
    weights = [(1 << 20) // math.isqrt(grade ** lean) + 1 for grade in range(1, number_of + 1)]
    largest = reach if full else min(reach, max(-(-total // number_of), total * weights[0] // sum(weights)))
    least = 1 if total - largest >= number_of - 1 else 0
    counts, rest = [largest] + [least] * (number_of - 1), total - largest - least * (number_of - 1)
    while rest > 0:
        free = [i for i in range(1, number_of) if counts[i] < largest] or [i for i in range(1, number_of) if counts[i] < reach]
        mass, left = sum([weights[i] for i in free]), rest
        for i in free:
            more = min(reach - counts[i], max(1, left * weights[i] // mass), rest)
            counts[i] = counts[i] + more
            rest = rest - more
    return np.array(counts)


def centred(rng, shape, scale, reach, shards=(), kind=jnp.bfloat16):
    entries = jax.random.normal(rng, shape, jnp.float32) * scale
    if len(shards) > 0:
        entries = levels(rng, shape, shards, -0.22, 0.18) * entries
    return jnp.clip(entries, min=-reach, max=reach).astype(kind)


def setup_inputs(seed: int = 0) -> dict:
    key_of = jax.random.split(jax.random.key(seed), 7)
    hidden_rows = centred(key_of[0], (ROWS, FFW), 1.0, 6.0, ((0, 16), (1, 8)))
    upstream = centred(key_of[1], (ROWS, D), 1.0, 6.0, ((0, 16),))
    advantages = centred(key_of[2], (N_FSDP, RPG), 1.0, 4.0, ((0, 16),), jnp.float32)
    lengths = jax.vmap(lambda own: uneven(own, RPG, S_DEV, MOSTLEN, 1))(jax.random.split(key_of[3], N_FSDP)).reshape((N_FSDP, RPG)).astype(jnp.int32)
    dest_rank_keys = jax.random.split(jax.random.fold_in(key_of[4], 1), BLOCKS_ALL // SRC_BLOCKS)
    dest_rank_turns = jax.random.permutation(jax.random.fold_in(key_of[4], 3), BLOCKS_ALL // SRC_BLOCKS)
    dest_rank = jax.vmap(lambda own, number: deal_out(jax.random.fold_in(key_of[4], 2), own, number, SRC_BLOCKS, N_FSDP, 1, SENDB, 2))(dest_rank_keys, dest_rank_turns).reshape((BLOCKS_ALL, 1))
    w_down = centred(key_of[5], (FFW, D), FFW ** -0.5, 0.046875, ((0, 8), (1, 16)))
    return {"hidden_rows": hidden_rows, "upstream": upstream, "advantages": advantages, "lengths": lengths, "dest_rank": dest_rank, "w_down": w_down}


def rounded(value):
    return lax.optimization_barrier(value.astype(jnp.bfloat16)).astype(jnp.float32)


def row_weights(advantages, lengths):
    ends_at = jnp.cumsum(lengths, axis=1)
    starts = ends_at - lengths
    position = jnp.arange(S_DEV, dtype=jnp.int32)[None, :, None]
    member = (position >= starts[:, None, :]) & (position < ends_at[:, None, :])
    factor = advantages * (S_DEV / (RPG * lengths.astype(jnp.float32)))
    weight = jnp.sum(jnp.where(member, factor[:, None, :], jnp.float32(0.0)), axis=2)
    return weight.reshape(N_FSDP * S_DEV)


def reference(hidden_rows, upstream, advantages, lengths, dest_rank, w_down):
    row_weight = row_weights(advantages, lengths)
    scaled = (row_weight[:, None] * upstream.astype(jnp.float32)).astype(jnp.bfloat16)
    width = FFW // N_DP

    def add_group(total, index):
        left = lax.dynamic_slice_in_dim(hidden_rows, index * width, width, 1)
        right = lax.dynamic_slice_in_dim(w_down, index * width, width, 0)
        return total + rounded(jnp.dot(left, right, preferred_element_type=jnp.float32)), None

    total, _ = lax.scan(add_group, jnp.zeros((N_FSDP * S_DEV, D), jnp.float32), jnp.arange(N_DP, dtype=jnp.int32))
    output_rows = total.astype(jnp.bfloat16)
    back_rows = lax.dot_general(scaled, w_down, (((1,), (1,)), ((), ())), preferred_element_type=jnp.float32).astype(jnp.bfloat16)

    def add_source(total, index):
        left = lax.dynamic_slice_in_dim(hidden_rows, index * S_DEV, S_DEV, 0)
        right = lax.dynamic_slice_in_dim(scaled, index * S_DEV, S_DEV, 0)
        part = lax.dot_general(left, right, (((0,), (0,)), ((), ())), preferred_element_type=jnp.float32)
        return total + rounded(part), None

    grads, _ = lax.scan(add_source, jnp.zeros((FFW, D), jnp.float32), jnp.arange(N_FSDP, dtype=jnp.int32))
    weight_grad = grads / (RPG * N_FSDP)

    block_rows = S_DEV // SRC_BLOCKS
    per_learner = N_FSDP * SENDB * block_rows
    target = dest_rank[:, 0].reshape(N_FSDP, SRC_BLOCKS)
    order = jnp.arange(SRC_BLOCKS, dtype=jnp.int32)
    earlier = order[None, :] < order[:, None]
    same = target[:, :, None] == target[:, None, :]
    slot_index = jnp.sum((same & earlier[None, :, :]).astype(jnp.int32), axis=2)
    group_ids = jnp.arange(N_FSDP, dtype=jnp.int32)[:, None]
    base = target * per_learner + (group_ids * SENDB + slot_index) * block_rows
    places = (base[:, :, None] + jnp.arange(block_rows, dtype=jnp.int32)[None, None, :]).reshape(-1)

    def place_rows(values):
        return jnp.zeros((per_learner * N_FSDP, values.shape[1]), values.dtype).at[places].set(values)

    return place_rows(output_rows), place_rows(back_rows), weight_grad
```

```python
import jax
import jax.numpy as jnp
from jax import lax
from jax.experimental import pallas as pl
from jax.experimental.pallas import tpu as pltpu
from jax.sharding import PartitionSpec as P

SENDB = 2
F32, BF16 = jnp.float32, jnp.bfloat16


def along(axis, step):
    if axis == "z":
        return [(4 * z + y, 4 * ((z + step) % 4) + y) for z in range(4) for y in range(4)]
    return [(4 * z + y, 4 * z + (y + step) % 4) for z in range(4) for y in range(4)]


def send(value, axis, step):
    return lax.ppermute(value, "fsdp", along(axis, step % 4))


def send_x(value, step):
    return lax.ppermute(
        value, "dp", [(2 * x + c, 2 * ((x + step) % 4) + c) for x in range(4) for c in range(2)]
    )


def send_core(value):
    return lax.ppermute(value, "dp", [(d, d ^ 1) for d in range(8)])


def send_turn(value):
    pairs = [
        ((2 * x + c) * 16 + 4 * z + y, (2 * z + c) * 16 + 4 * x + y)
        for x in range(4) for c in range(2) for z in range(4) for y in range(4)
    ]
    return lax.ppermute(value, ("dp", "fsdp"), pairs)


def scale_rows(place, advantages, lengths, upstream):
    rows = upstream.shape[0]
    width = upstream.shape[1] // 16

    def body(place_ref, adv_ref, len_ref, up_ref, *outs):
        row = lax.broadcasted_iota(jnp.int32, (rows, width), 0)
        weight = jnp.zeros((rows, width), F32)
        start = jnp.int32(0)
        for k in range(4):
            size = len_ref[0, k]
            inside = (row >= start) & (row < start + size)
            sized = jnp.full((rows, width), size, jnp.int32).astype(F32)
            weight = jnp.where(inside, adv_ref[0, k] * (rows / (4 * sized)), weight)
            start = start + size
        z, y = place_ref[2], place_ref[3]
        for q in range(4):
            for p in range(4):
                block = ((z + q) % 4) * 4 + (y + p) % 4
                part = up_ref[:, pl.ds(pl.multiple_of(block * width, width), width)]
                outs[q][:, p * width:(p + 1) * width] = (weight * part.astype(F32)).astype(BF16)

    smem = pl.BlockSpec(memory_space=pltpu.SMEM)
    vmem = pl.BlockSpec(memory_space=pltpu.VMEM)
    return pl.pallas_call(
        body,
        out_shape=[jax.ShapeDtypeStruct((rows, 4 * width), BF16)] * 4,
        in_specs=[smem, smem, smem, vmem],
        out_specs=[vmem] * 4,
        name="scale_rows",
    )(place, advantages, lengths, upstream)


def settle(place, parts, widths):
    def body(place_ref, *refs):
        ins, outs = refs[:4], refs[4:]
        z, y = place_ref[2], place_ref[3]
        for p in range(4):
            for q in range(4):
                at = pl.multiple_of((((z + 4 - q) % 4) * 4 + (y + 4 - p) % 4) * 16, 16)
                left = 0
                for out, width in zip(outs, widths):
                    out[pl.ds(at, 16), :] = ins[p][q * 16:(q + 1) * 16, left:left + width]
                    left += width

    smem = pl.BlockSpec(memory_space=pltpu.SMEM)
    vmem = pl.BlockSpec(memory_space=pltpu.VMEM)
    return pl.pallas_call(
        body,
        out_shape=[jax.ShapeDtypeStruct((256, width), BF16) for width in widths],
        in_specs=[smem] + [vmem] * 4,
        out_specs=[vmem] * len(widths),
        name="settle",
    )(place, *parts)


def ring_sum(parts, axis, halves):
    top, low = halves
    up_far = send(top(parts[2]), axis, 1)
    low_far = send(low(parts[2]), axis, -1)
    low_near = send(low(parts[1]), axis, 1)
    top_near = send(top(parts[3]), axis, -1)
    add = lambda a, b: (a.astype(F32) + b.astype(F32)).astype(BF16)
    top_sum = send(add(top(parts[1]), up_far), axis, 1)
    low_sum = send(add(low(parts[3]), low_far), axis, -1)
    three = lambda a, b, c: a.astype(F32) + b.astype(F32) + c.astype(F32)
    return three(top(parts[0]), top_sum, top_near), three(low(parts[0]), low_sum, low_near)


def on_device(hidden, upstream, advantages, lengths, dest_rank, w_down):
    d, f = lax.axis_index("dp"), lax.axis_index("fsdp")
    x, c, z, y = d // 2, d % 2, f // 4, f % 4
    place = jnp.stack([x, c, z, y]).astype(jnp.int32)
    rows, hid = hidden.shape
    half = hid // 2

    target = dest_rank[:, 0]
    order = jnp.arange(16, dtype=jnp.int32)
    same = target[:, None] == target[None, :]
    slot = jnp.sum((same & (order[None, :] < order[:, None])).astype(jnp.int32), axis=1)
    near = ((target // 4 - z) % 4) * 4 + (target % 4 - y) % 4
    at = ((near * SENDB + slot) * 8)[:, None] + jnp.arange(8, dtype=jnp.int32)[None, :]
    spread = (at.reshape(1, 128) == jnp.arange(256, dtype=jnp.int32)[:, None]).astype(BF16)

    scaled = scale_rows(place, advantages, lengths, upstream)
    w_top, w_low = w_down[:half], w_down[half:]
    w_top_b = send(w_top, "y", 1)
    w_low_f = send(w_low, "y", -1)
    s_1 = send(scaled[1], "z", 1)
    s_3 = send(scaled[3], "z", -1)
    h_1 = send(hidden, "z", 1)
    h_3 = send(hidden, "z", -1)
    s_2 = send(scaled[2], "z", 2)
    h_2 = send(hidden, "z", 2)
    w_low_b = send(w_low, "y", 1)
    w_top_f = send(w_top, "y", -1)
    w_top_2 = send(w_top_b, "y", 1)
    w_low_2 = send(w_low_f, "y", -1)

    h_all = jnp.concatenate([hidden, h_1, h_2, h_3], 0)
    s_all = jnp.concatenate([scaled[0], s_1, s_2, s_3], 0)
    w_1 = jnp.concatenate([w_top_f, w_low_f], 0)
    w_3 = jnp.concatenate([w_top_b, w_low_b], 0)
    w_2 = jnp.concatenate([w_top_2, w_low_2], 0)
    w_p = [w_down, w_1, w_2, w_3]

    g_p = [
        lax.dot_general(h_all, s_all[:, 256 * p:256 * (p + 1)], (((0,), (0,)), ((), ())), preferred_element_type=F32).astype(BF16)
        for p in range(4)
    ]
    g_top, g_low = ring_sum(g_p, "y", (lambda v: v[:half], lambda v: v[half:]))
    weight_grad = jnp.concatenate([g_top, g_low], 0) / 64

    w_all = jnp.concatenate(w_p, 1)
    b_all = lax.dot_general(s_all, w_all, (((1,), (1,)), ((), ())), preferred_element_type=F32).astype(BF16)
    b_i = [b_all[128 * i:128 * (i + 1)] for i in range(4)]
    b_top, b_low = ring_sum([b_i[0], b_i[3], b_i[2], b_i[1]], "z", (lambda v: v[:64], lambda v: v[64:]))
    back = jnp.concatenate([b_top.astype(BF16), b_low.astype(BF16)], 0)

    y_p = jnp.stack([jnp.dot(h_all, w, preferred_element_type=F32).astype(BF16) for w in w_p])
    y_p = y_p.reshape(4, 4, 128, 256)
    take = lambda v, k: lax.dynamic_index_in_dim(v, k, 0, keepdims=False)
    by_half = lambda k: jnp.stack([take(y_p, (2 * k - y) % 4), take(y_p, (2 * k + 1 - y) % 4)])
    mine, other = by_half(c), send_core(by_half(1 - c))
    pair = (mine.astype(F32) + other.astype(F32)).astype(BF16).transpose(1, 0, 2, 3)
    piece = lambda k: take(pair, (z - x - k) % 4)
    total = piece(0).astype(F32)
    for k in (1, 2, 3):
        total = total + send_x(piece(k), k).astype(F32)
    out_rows = send_turn(total.astype(BF16))
    out_rows = jnp.concatenate([out_rows[0], out_rows[1]], 1)

    both = jnp.concatenate([out_rows, back], 1)
    laid = jnp.dot(spread, both, preferred_element_type=F32).astype(BF16)
    got = [laid[:64]] + [send(laid[64 * q:64 * (q + 1)], "z", q) for q in (1, 2, 3)]
    to_y = lambda p: jnp.concatenate([g[16 * p:16 * (p + 1)] for g in got], 0)
    parts = [to_y(0)] + [send(to_y(p), "y", p) for p in (1, 2, 3)]
    packed_out, packed_back = settle(place, parts, (512, hid))
    return packed_out, packed_back, weight_grad


def solution(mesh):
    placed = (
        P("fsdp", "dp"), P("fsdp", None), P("fsdp", None), P("fsdp", None), P("fsdp", None), P("dp", "fsdp"),
    )
    return jax.shard_map(
        on_device, mesh=mesh, in_specs=placed,
        out_specs=(P("fsdp", "dp"), P("fsdp", "dp"), P("dp", "fsdp")), check_vma=False,
    )
```

```python
import jax
import jax.numpy as jnp
from jax import lax
from jax.experimental import pallas as pl
from jax.experimental.pallas import tpu as pltpu
from jax.sharding import PartitionSpec as P

SENDB = 2
F32, BF16 = jnp.float32, jnp.bfloat16
AXES = ("dp", "fsdp")


def pairs_of(move):
    at = lambda x, c, z, y: (2 * x + c) * 16 + 4 * z + y
    return [
        (at(x, c, z, y), at(*move(x, c, z, y)))
        for x in range(4) for c in range(2) for z in range(4) for y in range(4)
    ]


def along_a(step):
    return pairs_of(lambda x, c, z, y: (x, c, z, (y + step) % 4) if c else (x, c, (z + step) % 4, y))


def along_b(step):
    return pairs_of(lambda x, c, z, y: (x, c, (z + step) % 4, y) if c else (x, c, z, (y + step) % 4))


def send(value, pairs):
    return lax.ppermute(value, AXES, pairs)


def together(*values):
    return lax.optimization_barrier(values)


def scale_rows(place, advantages, lengths, upstream):
    rows = upstream.shape[0]
    width = upstream.shape[1] // 16

    def body(place_ref, adv_ref, len_ref, up_ref, *outs):
        row = lax.broadcasted_iota(jnp.int32, (rows, width), 0)
        weight = jnp.zeros((rows, width), F32)
        start = jnp.int32(0)
        for k in range(4):
            size = len_ref[0, k]
            inside = (row >= start) & (row < start + size)
            sized = jnp.full((rows, width), size, jnp.int32).astype(F32)
            weight = jnp.where(inside, adv_ref[0, k] * (rows / (4 * sized)), weight)
            start = start + size
        c, a, b = place_ref[1], place_ref[2], place_ref[3]
        for q in range(4):
            for p in range(4):
                far, near = (a + q) % 4, (b + p) % 4
                block = jnp.where(c == 0, 4 * far + near, 4 * near + far)
                part = up_ref[:, pl.ds(pl.multiple_of(block * width, width), width)]
                outs[q][:, p * width:(p + 1) * width] = (weight * part.astype(F32)).astype(BF16)

    smem = pl.BlockSpec(memory_space=pltpu.SMEM)
    vmem = pl.BlockSpec(memory_space=pltpu.VMEM)
    return pl.pallas_call(
        body,
        out_shape=[jax.ShapeDtypeStruct((rows, 4 * width), BF16)] * 4,
        in_specs=[smem, smem, smem, vmem],
        out_specs=[vmem] * 4,
        compiler_params=pltpu.CompilerParams(vmem_limit_bytes=8 << 20),
        name="scale_rows",
    )(place, advantages, lengths, upstream)


SMEM = pl.BlockSpec(memory_space=pltpu.SMEM)
VMEM = pl.BlockSpec(memory_space=pltpu.VMEM)


def shaped(*shape):
    return jax.ShapeDtypeStruct(shape, BF16)


def limit(mib):
    return pltpu.CompilerParams(vmem_limit_bytes=mib << 20)


TILE = 384


def stacked(refs, dim):
    return jnp.concatenate([ref[...] for ref in refs], dim)


def row_blocks(pieces, block, at):
    return [pl.BlockSpec((piece.shape[0], block), at) for piece in pieces]


def back_rows(scaled, weights):
    rows, feats = scaled[0].shape
    hid = weights[0].shape[0]
    n_w = len(weights)

    def body(*refs):
        s, w, outs, full = refs[:4], refs[4:4 + n_w], refs[4 + n_w:8 + n_w], refs[8 + n_w]

        @pl.when(pl.program_id(0) == 0)
        def _():
            for i in range(4):
                full[i * rows:(i + 1) * rows, :] = s[i][...]

        total = lax.dot_general(full[...], stacked(w, 1), (((1,), (1,)), ((), ())), preferred_element_type=F32)
        for i in range(4):
            outs[i][...] = total[i * rows:(i + 1) * rows].astype(BF16)

    return pl.pallas_call(
        body,
        grid=(hid // TILE,),
        out_shape=[shaped(rows, hid)] * 4,
        in_specs=[pl.BlockSpec((rows, feats), lambda n: (0, 0))] * 4
        + [pl.BlockSpec((TILE, w.shape[1]), lambda n: (n, 0)) for w in weights],
        out_specs=[pl.BlockSpec((rows, TILE), lambda n: (0, n))] * 4,
        scratch_shapes=[pltpu.VMEM((4 * rows, feats), BF16)],
        compiler_params=limit(16),
        name="back_rows",
    )(*scaled, *weights)


def weight_parts(hidden, scaled):
    rows, feats = scaled[0].shape
    hid = hidden[0].shape[1]
    width = feats // 4
    n_h = len(hidden)

    def body(*refs):
        h, s, outs, full = refs[:n_h], refs[n_h:n_h + 4], refs[n_h + 4:n_h + 8], refs[n_h + 8]

        @pl.when(pl.program_id(0) == 0)
        def _():
            for i in range(4):
                full[i * rows:(i + 1) * rows, :] = s[i][...]

        left = stacked(h, 0)
        for p in range(4):
            outs[p][...] = lax.dot_general(
                left, full[:, p * width:(p + 1) * width], (((0,), (0,)), ((), ())), preferred_element_type=F32).astype(BF16)

    return pl.pallas_call(
        body,
        grid=(hid // TILE,),
        out_shape=[shaped(hid, width)] * 4,
        in_specs=row_blocks(hidden, TILE, lambda n: (0, n)) + [pl.BlockSpec((rows, feats), lambda n: (0, 0))] * 4,
        out_specs=[pl.BlockSpec((TILE, width), lambda n: (n, 0))] * 4,
        scratch_shapes=[pltpu.VMEM((4 * rows, feats), BF16)],
        compiler_params=limit(16),
        name="weight_parts",
    )(*hidden, *scaled)


def out_parts(place, hidden, weights):
    hid = hidden[0].shape[1]
    rows = 128
    width = 256
    n_h, n_w = len(hidden), len(weights)

    def body(place_ref, *refs):
        h, w, outs = refs[:n_h], refs[n_h:n_h + n_w], refs[n_h + n_w:n_h + n_w + 4]
        left, total = refs[n_h + n_w + 4:]
        step = pl.program_id(0)

        @pl.when(step == 0)
        def _():
            start = 0
            for ref in h:
                left[start:start + ref.shape[0], :] = ref[...]
                start += ref.shape[0]

        part = jnp.dot(left[pl.ds(pl.multiple_of(step * rows, rows), rows), :], stacked(w, 1), preferred_element_type=F32).astype(BF16)
        for p in range(4):
            total[p, step] = part[:, p * width:(p + 1) * width]

        @pl.when(step == 3)
        def _():
            x, c, a, b = place_ref[0], place_ref[1], place_ref[2], place_ref[3]
            for k in range(4):
                group, block = (a - x - k + 8) % 4, (x + k - b + 8) % 4
                for u in range(4):
                    i = jnp.where(c == 0, group, u)
                    p = jnp.where(c == 0, u, block)
                    outs[k][u] = total[p, i]

    whole = lambda v: pl.BlockSpec(v.shape, lambda n: (0, 0), pipeline_mode=pl.Buffered(1))
    return pl.pallas_call(
        body,
        grid=(4,),
        out_shape=[shaped(4, rows, width)] * 4,
        in_specs=[SMEM] + [whole(v) for v in hidden] + [whole(w) for w in weights],
        out_specs=[pl.BlockSpec((4, rows, width), lambda n: (0, 0, 0))] * 4,
        scratch_shapes=[pltpu.VMEM((4 * rows, hid), BF16), pltpu.VMEM((4, 4, rows, width), BF16)],
        compiler_params=limit(24),
        name="out_parts",
    )(place, *hidden, *weights)


def out_turn(place, own, got):
    _, rows, width = own.shape

    def body(place_ref, own_ref, g1, g2, g3, t0, t1, t2, t3):
        c, y = place_ref[1], place_ref[4]

        def total(u):
            return (own_ref[u].astype(F32) + g1[u].astype(F32) + g2[u].astype(F32) + g3[u].astype(F32)).astype(BF16)

        for j, out in enumerate((t0, t1, t2, t3)):
            half = 1 - ((y + j) % 4) // 2
            if j % 2:
                out[...] = total(j)
            else:
                out[:, :width] = total(jnp.where(c == 0, (2 * half - y + 4) % 4, j))
                out[:, width:] = total((2 * half + 1 - y + 4) % 4)

    return pl.pallas_call(
        body,
        out_shape=[shaped(rows, 2 * width), shaped(rows, width), shaped(rows, 2 * width), shaped(rows, width)],
        in_specs=[SMEM] + [VMEM] * 4,
        out_specs=[VMEM] * 4,
        compiler_params=limit(8),
        name="out_turn",
    )(place, own, *got)


def lay_rows(place, spread, turned, own, got):
    _, hid = own.shape
    width = turned[1].shape[1]

    def body(place_ref, spread_ref, t0, t1, t2, t3, b0, b1, b2, b3, out_ref):
        c, y = place_ref[1], place_ref[4]
        near = jnp.where(1 - y // 2 == c, t0[...].astype(F32), t2[...].astype(F32))
        sides = []
        for h in range(2):
            j = (2 * c + h - y + 4) % 4
            side = t0[:, :width].astype(F32)
            for n, ref in ((1, t1), (2, t2), (3, t3)):
                side = jnp.where(j == n, ref[:, :width].astype(F32), side)
            sides.append((near[:, h * width:(h + 1) * width] + side).astype(BF16))
        lay = spread_ref[...]
        out_ref[:, :2 * width] = jnp.dot(lay, jnp.concatenate(sides, 1), preferred_element_type=F32).astype(BF16)
        back = (b0[...].astype(F32) + b1[...].astype(F32) + b2[...].astype(F32) + b3[...].astype(F32)).astype(BF16)
        out_ref[:, 2 * width:] = jnp.dot(lay, back, preferred_element_type=F32).astype(BF16)

    slots = spread.shape[0]
    return pl.pallas_call(
        body,
        out_shape=shaped(slots, 2 * width + hid),
        in_specs=[SMEM] + [VMEM] * 9,
        out_specs=VMEM,
        compiler_params=limit(16),
        name="lay_rows",
    )(place, spread, *turned, own, *got)


def layer(hidden, upstream, advantages, lengths, dest_rank, w_down):
    d, f = lax.axis_index("dp"), lax.axis_index("fsdp")
    x, c, z, y = d // 2, d % 2, f // 4, f % 4
    a, b = jnp.where(c == 0, z, y), jnp.where(c == 0, y, z)
    place = jnp.stack([x, c, a, b, y]).astype(jnp.int32)

    target = dest_rank[:, 0]
    order = jnp.arange(16, dtype=jnp.int32)
    same = target[:, None] == target[None, :]
    slot = jnp.sum((same & (order[None, :] < order[:, None])).astype(jnp.int32), axis=1)
    at = ((target * SENDB + slot) * 8)[:, None] + jnp.arange(8, dtype=jnp.int32)[None, :]
    spread = (at.reshape(1, 128) == jnp.arange(256, dtype=jnp.int32)[:, None]).astype(BF16)

    h_1, h_3 = send(hidden, along_a(1)), send(hidden, along_a(-1))
    scaled = scale_rows(place, advantages, lengths, upstream)
    s_all = [scaled[0], send(scaled[1], along_a(1)), send(scaled[2], along_a(2)), send(scaled[3], along_a(-1))]
    w_3, w_1 = send(w_down, along_b(1)), send(w_down, along_b(-1))
    middle = hidden.shape[0] // 2
    h_top, h_low = send(h_1[:middle], along_a(1)), send(h_3[middle:], along_a(-1))
    h_all = [hidden, h_1, h_top, h_low, h_3]

    g_p = list(weight_parts(h_all, s_all))
    w_1, w_3, *g_p = together(w_1, w_3, *g_p)
    half = w_down.shape[1] // 2
    w_left, w_right = send(w_3[:, :half], along_b(1)), send(w_1[:, half:], along_b(-1))
    w_all = [w_down, w_1, w_left, w_right, w_3]
    got_g = [send(g_p[2], along_b(2)), send(g_p[1], along_b(1)), send(g_p[3], along_b(-1))]

    y_k = list(out_parts(place, h_all, w_all))
    got_y = [send(y_k[k], pairs_of(lambda x, c, z, y: ((x + k) % 4, c, z, y))) for k in (2, 1, 3)]

    *s_all, y_k[0] = together(*s_all, y_k[0])
    b_i = list(back_rows(s_all, w_all))
    got_b = [send(b_i[2], along_a(2)), send(b_i[3], along_a(1)), send(b_i[1], along_a(-1))]

    turned = []
    for j, value in enumerate(out_turn(place, y_k[0], got_y)):
        def home(x, c, z, y):
            if c:
                return x, y // 2, z, (y - j) % 4
            return z, 1 - ((y + j) % 4) // 2, x, y

        moves = pairs_of(home)
        if j % 2:
            moves = [(one, two) for one, two in moves if one // 16 % 2]
        turned.append(send(value, moves))

    laid = lay_rows(place, spread, turned, b_i[0], got_b).reshape(16, 16, -1)
    packed = lax.all_to_all(laid, "fsdp", split_axis=0, concat_axis=0, tiled=True).reshape(256, -1)
    weight_grad = (g_p[0].astype(F32) + got_g[0].astype(F32) + got_g[1].astype(F32) + got_g[2].astype(F32)) / 64
    return packed[:, :512], packed[:, 512:], weight_grad


def solution(mesh):
    placed = (
        P("fsdp", "dp"), P("fsdp", None), P("fsdp", None), P("fsdp", None), P("fsdp", None), P("dp", "fsdp"),
    )
    return jax.shard_map(
        layer, mesh=mesh, in_specs=placed,
        out_specs=(P("fsdp", "dp"), P("fsdp", "dp"), P("dp", "fsdp")), check_vma=False,
    )
```

```python
import jax
import jax.numpy as jnp
from jax import lax
from jax.experimental import pallas as pl
from jax.experimental.pallas import tpu as pltpu
from jax.sharding import PartitionSpec as P

SENDB = 2
F32, BF16 = jnp.float32, jnp.bfloat16
AXES = ("dp", "fsdp")


def pairs_of(move):
    at = lambda x, c, z, y: (2 * x + c) * 16 + 4 * z + y
    return [
        (at(x, c, z, y), at(*move(x, c, z, y)))
        for x in range(4) for c in range(2) for z in range(4) for y in range(4)
    ]


def along_a(step):
    return pairs_of(lambda x, c, z, y: (x, c, z, (y + step) % 4) if c else (x, c, (z + step) % 4, y))


def along_b(step):
    return pairs_of(lambda x, c, z, y: (x, c, (z + step) % 4, y) if c else (x, c, z, (y + step) % 4))


def send(value, pairs):
    return lax.ppermute(value, AXES, pairs)


def scale_rows(place, advantages, lengths, upstream):
    rows = upstream.shape[0]
    width = upstream.shape[1] // 16

    def body(place_ref, adv_ref, len_ref, up_ref, *outs):
        row = lax.broadcasted_iota(jnp.int32, (rows, width), 0)
        weight = jnp.zeros((rows, width), F32)
        start = jnp.int32(0)
        for k in range(4):
            size = len_ref[0, k]
            inside = (row >= start) & (row < start + size)
            sized = jnp.full((rows, width), size, jnp.int32).astype(F32)
            weight = jnp.where(inside, adv_ref[0, k] * (rows / (4 * sized)), weight)
            start = start + size
        c, a, b = place_ref[1], place_ref[2], place_ref[3]
        for q in range(4):
            for p in range(4):
                far, near = (a + q) % 4, (b + p) % 4
                block = jnp.where(c == 0, 4 * far + near, 4 * near + far)
                part = up_ref[:, pl.ds(pl.multiple_of(block * width, width), width)]
                outs[q][:, p * width:(p + 1) * width] = (weight * part.astype(F32)).astype(BF16)

    smem = pl.BlockSpec(memory_space=pltpu.SMEM)
    vmem = pl.BlockSpec(memory_space=pltpu.VMEM)
    return pl.pallas_call(
        body,
        out_shape=[jax.ShapeDtypeStruct((rows, 4 * width), BF16)] * 4,
        in_specs=[smem, smem, smem, vmem],
        out_specs=[vmem] * 4,
        compiler_params=pltpu.CompilerParams(vmem_limit_bytes=8 << 20),
        name="scale_rows",
    )(place, advantages, lengths, upstream)


SMEM = pl.BlockSpec(memory_space=pltpu.SMEM)
VMEM = pl.BlockSpec(memory_space=pltpu.VMEM)


def shaped(*shape):
    return jax.ShapeDtypeStruct(shape, BF16)


def limit(mib):
    return pltpu.CompilerParams(vmem_limit_bytes=mib << 20)


TILE = 640


def stacked(refs, dim):
    return jnp.concatenate([ref[...] for ref in refs], dim)


def row_blocks(pieces, block, at):
    return [pl.BlockSpec((piece.shape[0], block), at) for piece in pieces]


def back_rows(scaled, weights):
    rows, feats = scaled[0].shape
    hid = weights[0].shape[0]
    n_w = len(weights)

    def body(*refs):
        s, w, outs, full = refs[:4], refs[4:4 + n_w], refs[4 + n_w:8 + n_w], refs[8 + n_w]

        @pl.when(pl.program_id(0) == 0)
        def _():
            for i in range(4):
                full[i * rows:(i + 1) * rows, :] = s[i][...]

        total = lax.dot_general(full[...], stacked(w, 1), (((1,), (1,)), ((), ())), preferred_element_type=F32)
        for i in range(4):
            outs[i][...] = total[i * rows:(i + 1) * rows].astype(BF16)

    return pl.pallas_call(
        body,
        grid=(hid // TILE,),
        out_shape=[shaped(rows, hid)] * 4,
        in_specs=[pl.BlockSpec((rows, feats), lambda n: (0, 0))] * 4
        + [pl.BlockSpec((TILE, w.shape[1]), lambda n: (n, 0)) for w in weights],
        out_specs=[pl.BlockSpec((rows, TILE), lambda n: (0, n))] * 4,
        scratch_shapes=[pltpu.VMEM((4 * rows, feats), BF16)],
        compiler_params=limit(16),
        name="back_rows",
    )(*scaled, *weights)


def weight_parts(hidden, scaled):
    rows, feats = scaled[0].shape
    hid = hidden[0].shape[1]
    width = feats // 4
    n_h = len(hidden)

    def body(*refs):
        h, s, outs, full = refs[:n_h], refs[n_h:n_h + 4], refs[n_h + 4:n_h + 8], refs[n_h + 8]

        @pl.when(pl.program_id(0) == 0)
        def _():
            for i in range(4):
                full[i * rows:(i + 1) * rows, :] = s[i][...]

        left = stacked(h, 0)
        for p in range(4):
            outs[p][...] = lax.dot_general(
                left, full[:, p * width:(p + 1) * width], (((0,), (0,)), ((), ())), preferred_element_type=F32).astype(BF16)

    return pl.pallas_call(
        body,
        grid=(hid // TILE,),
        out_shape=[shaped(hid, width)] * 4,
        in_specs=row_blocks(hidden, TILE, lambda n: (0, n)) + [pl.BlockSpec((rows, feats), lambda n: (0, 0))] * 4,
        out_specs=[pl.BlockSpec((TILE, width), lambda n: (n, 0))] * 4,
        scratch_shapes=[pltpu.VMEM((4 * rows, feats), BF16)],
        compiler_params=limit(16),
        name="weight_parts",
    )(*hidden, *scaled)


def out_parts(place, hidden, weights):
    hid = hidden[0].shape[1]
    rows = 128
    width = 256
    n_h, n_w = len(hidden), len(weights)

    def body(place_ref, *refs):
        h, w, outs = refs[:n_h], refs[n_h:n_h + n_w], refs[n_h + n_w:n_h + n_w + 4]
        left, total = refs[n_h + n_w + 4:]
        step = pl.program_id(0)

        @pl.when(step == 0)
        def _():
            start = 0
            for ref in h:
                left[start:start + ref.shape[0], :] = ref[...]
                start += ref.shape[0]

        part = jnp.dot(left[pl.ds(pl.multiple_of(step * rows, rows), rows), :], stacked(w, 1), preferred_element_type=F32).astype(BF16)
        for p in range(4):
            total[p, step] = part[:, p * width:(p + 1) * width]

        @pl.when(step == 3)
        def _():
            x, c, a, b = place_ref[0], place_ref[1], place_ref[2], place_ref[3]
            for k in range(4):
                group, block = (a - x - k + 8) % 4, (x + k - b + 8) % 4
                for u in range(4):
                    i = jnp.where(c == 0, group, u)
                    p = jnp.where(c == 0, u, block)
                    outs[k][u] = total[p, i]

    whole = lambda v: pl.BlockSpec(v.shape, lambda n: (0, 0), pipeline_mode=pl.Buffered(1))
    return pl.pallas_call(
        body,
        grid=(4,),
        out_shape=[shaped(4, rows, width)] * 4,
        in_specs=[SMEM] + [whole(v) for v in hidden] + [whole(w) for w in weights],
        out_specs=[pl.BlockSpec((4, rows, width), lambda n: (0, 0, 0))] * 4,
        scratch_shapes=[pltpu.VMEM((4 * rows, hid), BF16), pltpu.VMEM((4, 4, rows, width), BF16)],
        compiler_params=limit(24),
        name="out_parts",
    )(place, *hidden, *weights)


def out_turn(own, got):
    _, rows, width = own.shape

    def body(own_ref, g1, g2, g3, all_ref, *one_refs):
        for u in range(4):
            total = (own_ref[u].astype(F32) + g1[u].astype(F32) + g2[u].astype(F32) + g3[u].astype(F32)).astype(BF16)
            all_ref[:, u * width:(u + 1) * width] = total
            if u:
                one_refs[u - 1][...] = total

    return pl.pallas_call(
        body,
        out_shape=[shaped(rows, 4 * width)] + [shaped(rows, width)] * 3,
        in_specs=[VMEM] * 4,
        out_specs=[VMEM] * 4,
        compiler_params=limit(8),
        name="out_turn",
    )(own, *got)


def out_swap(place, own, turned, ones):
    rows, width = ones[0].shape

    def body(place_ref, own_ref, all_ref, r1, r2, r3, mine_ref, other_ref):
        c, y = place_ref[1], place_ref[4]
        for out, core in ((mine_ref, c), (other_ref, 1 - c)):
            for h in range(2):
                j = (2 * core + h - y + 4) % 4
                at = pl.ds(h * width, width)

                @pl.when(c == 0)
                def _():
                    out[:, at] = all_ref[:, pl.ds(pl.multiple_of(j * width, width), width)]

                for n, ref in enumerate((own_ref, r1, r2, r3)):
                    @pl.when((c == 1) & (j == n))
                    def _():
                        out[:, at] = ref[:, :width]

    return pl.pallas_call(
        body,
        out_shape=[shaped(rows, 2 * width)] * 2,
        in_specs=[SMEM] + [VMEM] * 5,
        out_specs=[VMEM] * 2,
        compiler_params=limit(8),
        name="out_swap",
    )(place, own, turned, *ones)


def lay_rows(spread, shares):
    _, feats = shares[0].shape

    def body(spread_ref, *refs):
        ins, outs = refs[:len(shares)], refs[len(shares):]
        total = ins[0][...].astype(F32)
        for ref in ins[1:]:
            total = total + ref[...].astype(F32)
        laid = jnp.dot(spread_ref[...], total.astype(BF16), preferred_element_type=F32).astype(BF16)
        for q in range(4):
            outs[q][...] = laid[64 * q:64 * (q + 1)]

    return pl.pallas_call(
        body,
        out_shape=[shaped(64, feats)] * 4,
        in_specs=[VMEM] * (1 + len(shares)),
        out_specs=[VMEM] * 4,
        compiler_params=limit(16),
    )(spread, *shares)


def regroup(out_parts, back_parts):
    feats, hid = out_parts[0].shape[1], back_parts[0].shape[1]

    def body(*refs):
        for q in range(4):
            for p in range(4):
                rows, into = slice(16 * p, 16 * (p + 1)), slice(16 * q, 16 * (q + 1))
                refs[8 + p][into, :feats] = refs[q][rows, :]
                refs[8 + p][into, feats:] = refs[4 + q][rows, :]

    return pl.pallas_call(
        body,
        out_shape=[shaped(64, feats + hid)] * 4,
        in_specs=[VMEM] * 8,
        out_specs=[VMEM] * 4,
        compiler_params=limit(8),
        name="regroup",
    )(*out_parts, *back_parts)


def settle(place, parts, widths):
    def body(place_ref, *refs):
        ins, outs = refs[:4], refs[4:]
        c, a, b = place_ref[1], place_ref[2], place_ref[3]
        for p in range(4):
            for q in range(4):
                far, near = (a + 4 - q) % 4, (b + 4 - p) % 4
                group = jnp.where(c == 0, 4 * far + near, 4 * near + far)
                at = pl.ds(pl.multiple_of(group * 16, 16), 16)
                left = 0
                for out, width in zip(outs, widths):
                    out[at, :] = ins[p][q * 16:(q + 1) * 16, left:left + width]
                    left += width

    return pl.pallas_call(
        body,
        out_shape=[shaped(256, width) for width in widths],
        in_specs=[SMEM] + [VMEM] * 4,
        out_specs=[VMEM] * len(widths),
        compiler_params=limit(8),
        name="settle",
    )(place, *parts)


def layer(hidden, upstream, advantages, lengths, dest_rank, w_down):
    d, f = lax.axis_index("dp"), lax.axis_index("fsdp")
    x, c, z, y = d // 2, d % 2, f // 4, f % 4
    a, b = jnp.where(c == 0, z, y), jnp.where(c == 0, y, z)
    place = jnp.stack([x, c, a, b, y]).astype(jnp.int32)

    target = dest_rank[:, 0]
    order = jnp.arange(16, dtype=jnp.int32)
    same = target[:, None] == target[None, :]
    slot = jnp.sum((same & (order[None, :] < order[:, None])).astype(jnp.int32), axis=1)
    target_a = jnp.where(c == 0, target // 4, target % 4)
    target_b = jnp.where(c == 0, target % 4, target // 4)
    near = ((target_a - a) % 4) * 4 + (target_b - b) % 4
    at = ((near * SENDB + slot) * 8)[:, None] + jnp.arange(8, dtype=jnp.int32)[None, :]
    spread = (at.reshape(1, 128) == jnp.arange(256, dtype=jnp.int32)[:, None]).astype(BF16)

    h_1, h_3 = send(hidden, along_a(1)), send(hidden, along_a(-1))
    scaled = scale_rows(place, advantages, lengths, upstream)
    s_all = [scaled[0], send(scaled[1], along_a(1)), send(scaled[2], along_a(2)), send(scaled[3], along_a(-1))]
    w_3, w_1 = send(w_down, along_b(1)), send(w_down, along_b(-1))
    middle = hidden.shape[0] // 2
    h_top, h_low = send(h_1[:middle], along_a(1)), send(h_3[middle:], along_a(-1))
    h_all = [hidden, h_1, h_top, h_low, h_3]

    g_p = list(weight_parts(h_all, s_all))
    half = w_down.shape[1] // 2
    w_left, w_right = send(w_3[:, :half], along_b(1)), send(w_1[:, half:], along_b(-1))
    w_all = [w_down, w_1, w_left, w_right, w_3]
    got_g = [send(g_p[2], along_b(2)), send(g_p[1], along_b(1)), send(g_p[3], along_b(-1))]

    y_k = list(out_parts(place, h_all, w_all))
    got_y = [send(y_k[k], pairs_of(lambda x, c, z, y: ((x + k) % 4, c, z, y))) for k in (2, 1, 3)]

    b_i = list(back_rows(s_all, w_all))
    got_b = [send(b_i[2], along_a(2)), send(b_i[3], along_a(1)), send(b_i[1], along_a(-1))]

    own_out, *ones = out_turn(y_k[0], got_y)
    only = lambda core, pairs: [(one, two) for one, two in pairs if one // 16 % 2 == core]
    turned = send(own_out, only(0, pairs_of(lambda x, c, z, y: (z, c, x, y))))
    ones = [send(one, only(1, pairs_of(lambda x, c, z, y: (x, c, z, (y - j) % 4)))) for j, one in enumerate(ones, 1)]

    def along(laid):
        far, near, back = send(laid[2], along_a(2)), send(laid[1], along_a(1)), send(laid[3], along_a(-1))
        return [laid[0], near, far, back]

    back = along(lay_rows(spread, [b_i[0], *got_b]))
    mine, other = out_swap(place, own_out, turned, ones)
    other = send(other, pairs_of(lambda x, c, z, y: (x, 1 - c, z, y)))
    out = along(lay_rows(spread, [mine, other]))
    dealt = regroup(out, back)
    parts = [dealt[0]] + [send(dealt[p], along_b(p)) for p in (1, 2, 3)]
    packed_out, packed_back = settle(place, parts, (512, w_down.shape[0]))
    weight_grad = (g_p[0].astype(F32) + got_g[0].astype(F32) + got_g[1].astype(F32) + got_g[2].astype(F32)) / 64
    return packed_out, packed_back, weight_grad


def solution(mesh):
    placed = (
        P("fsdp", "dp"), P("fsdp", None), P("fsdp", None), P("fsdp", None), P("fsdp", None), P("dp", "fsdp"),
    )
    return jax.shard_map(
        layer, mesh=mesh, in_specs=placed,
        out_specs=(P("fsdp", "dp"), P("fsdp", "dp"), P("dp", "fsdp")), check_vma=False,
    )
```
